32 devices in a mesh: groups: 2 (over x), example: 8 (over z, y), cls: 2 (over core).
Axes of the slice: x: 2, y: 2, z: 4, core: 2. Of those that a mesh axis runs over, the one named last changes fastest.
Arguments:
- features: bfloat16 [2048, 4096], P(('groups', 'example'), 'cls'), parts along dimension 0
- weights: float32 [8192, 8192], P(('groups', 'cls'), 'example'), parts along dimension 0
- labels: int32 [2048], P(('groups', 'example')), parts along dimension 0, may hold values from 0 to 8191
- counts: int32 [16], P(('groups', 'example')), parts along dimension 0, may hold values from 16 to 128, as said below
- active: int32 [2], P('groups'), parts along dimension 0, may hold values from 4096 to 8192
Outputs:
- moved: float32 [8192, 8192], P(('groups', 'cls'), 'example'), parts along dimension 0
- losses: float32 [2048], P(('groups', 'example')), parts along dimension 0
The draws below stay inside these ranges and needn't reach their ends.
There are 2 independent parts, one for each index of `groups`. The reference program is written for one: setup_inputs(seed, part) draws one part's arguments, and reference() takes and returns one part's arrays. A program takes and returns all parts, laid end to end along the dimension named above; each array names one. Nothing has to cross between parts.
Inputs may be any that keep to these rules, and one draw needn't show every extreme that they name: `counts`: each block has at least 16 valid slots; some block is full in every draw.
All inputs are finite; a program needn't handle non-finite values.
Results may differ from the reference program's by a relative error of at most 0.006.
Values may be sent and summed in bfloat16 or wider, within the bound.
A program may use at most 128 MiB of HBM per device.

```python
import math
import jax
import jax.numpy as jnp
import numpy as np

FEATURES = 4096
CLASSES = 8192
EX_DEV = 128
ITERS = 2
EXAMPLES = 1024


def draw_features(key, part):
    feature_pos = jnp.arange(FEATURES).astype(jnp.float32) / FEATURES
    rough = jnp.exp(jax.random.uniform(jax.random.fold_in(key, 1), (FEATURES,), jnp.float32, jnp.log(0.7), jnp.log(1.4)))
    col_scale = 0.4 * jnp.power(10.0, feature_pos) * rough
    row_scale = jnp.exp(jax.random.uniform(jax.random.fold_in(key, 2), (EXAMPLES, 1), jnp.float32, jnp.log(0.6), jnp.log(1.6)))
    base = jax.random.truncated_normal(jax.random.fold_in(key, 3), -4.0, 4.0, (EXAMPLES, FEATURES), jnp.float32)
    values = base * row_scale * col_scale
    return values.astype(jnp.bfloat16)


def draw_weights(key, part):
    class_scale = jnp.exp(jax.random.uniform(jax.random.fold_in(key, 21), (1, CLASSES), jnp.float32, jnp.log(0.5), jnp.log(5.0)))
    base = jax.random.truncated_normal(jax.random.fold_in(key, 22), -4.0, 4.0, (FEATURES, CLASSES), jnp.float32)
    values = base * class_scale / jnp.sqrt(float(FEATURES))
    return values


def draw_counts(key, part):
    blocks = EXAMPLES // EX_DEV
    lowest = max(EX_DEV // 8, 1)
    first_draw = jax.random.randint(jax.random.fold_in(key, 31), (blocks,), lowest, EX_DEV + 1)
    second_draw = jax.random.randint(jax.random.fold_in(key, 32), (blocks,), lowest, EX_DEV + 1)
    full_block = jax.random.randint(jax.random.fold_in(key, 33), (), 0, blocks)
    values = jnp.minimum(first_draw, second_draw)
    return jnp.where(jnp.arange(blocks) == full_block, EX_DEV, values).astype(jnp.int32)


def plant(drawn, rng, low, top_value):
    longest = drawn.shape.index(max(drawn.shape))
    spots = []
    for shift in (0, 1):
        where = [jax.random.randint(jax.random.fold_in(rng, axis), (), 0, length) for axis, length in enumerate(drawn.shape)]
        where[longest] = (where[longest] + shift) % drawn.shape[longest]
        spots.append(tuple(where))
    return drawn.at[spots[0]].set(low).at[spots[1]].set(top_value)


def cumulative_ranks(amount, skew):
    weights = [(1 << 20) // math.isqrt(rank ** skew) + 1 for rank in range(1, amount + 1)]
    spread = 1 + sum(weights) // (1 << 30)
    return np.cumsum(np.array([max(1, weight // spread) for weight in weights]))


def skewed_ids(own_key, dims, amount, slope):
    grid = cumulative_ranks(amount, slope)
    lot = jax.random.randint(jax.random.fold_in(own_key, 1), dims, 0, int(grid[amount - 1]))
    grade = jnp.searchsorted(jnp.asarray(grid, jnp.int32), lot, side="right")
    return jax.random.permutation(jax.random.fold_in(own_key, 2), amount)[grade].astype(jnp.int32)


def setup_inputs(seed: int = 0, part: int = 0) -> dict:
    arg_keys = jax.random.split(jax.random.key(seed), 6)
    part_keys = jax.random.split(jax.random.fold_in(arg_keys[5], part), 6)
    features = draw_features(jax.random.fold_in(jax.random.fold_in(arg_keys[5], part), 71), part)
    weights = draw_weights(jax.random.fold_in(jax.random.fold_in(arg_keys[5], part), 71), part)
    labels = plant(skewed_ids(part_keys[2], (EXAMPLES,), CLASSES, 2), jax.random.fold_in(part_keys[2], 3), 0, CLASSES - 1).astype(jnp.int32)
    counts = draw_counts(jax.random.fold_in(jax.random.fold_in(arg_keys[5], part), 71), part)
    active = jax.random.randint(part_keys[4], (1,), CLASSES // 2, CLASSES + 1).astype(jnp.int32)
    return {"features": features, "weights": weights, "labels": labels, "counts": counts, "active": active}


NEGATIVE = -1e30
LEARNING_RATE = 2e-5
DAMPING_SHARE = 0.1
EPSILON = 1e-6


def reference(features, weights, labels, counts, active):
    row_index = jnp.arange(EXAMPLES)
    is_valid = ((row_index % EX_DEV) < counts[row_index // EX_DEV]).astype(jnp.float32)
    valid_total = jnp.sum(counts).astype(jnp.float32)
    active_count = active[0]
    target = (labels % active_count).astype(jnp.int32)
    class_index = jnp.arange(CLASSES)
    is_active = class_index < active_count
    is_label = class_index[None, :] == target[:, None]
    squares = (features.astype(jnp.float32) * features.astype(jnp.float32)).astype(jnp.bfloat16)
    current = weights
    moved = jnp.zeros_like(weights)
    denominator = None
    losses = None
    for iteration in range(ITERS):
        current_low = current.astype(jnp.bfloat16)
        logits = jnp.dot(features, current_low, preferred_element_type=jnp.float32)
        masked = jnp.where(is_active[None, :], logits, NEGATIVE)
        row_peak = jnp.max(masked, axis=1)
        exponent = jnp.exp(masked - row_peak[:, None])
        row_total = jnp.sum(exponent, axis=1)
        label_logit = jnp.sum(jnp.where(is_label, logits, 0.0), axis=1)
        probability = exponent / row_total[:, None]
        residual = (is_valid[:, None] * (probability - is_label.astype(jnp.float32)) / valid_total).astype(jnp.bfloat16)
        gradient = jnp.dot(features.T, residual, preferred_element_type=jnp.float32)
        if iteration == 0:
            fisher_weight = (is_valid[:, None] * probability * (1.0 - probability) / valid_total).astype(jnp.bfloat16)
            fisher = jnp.dot(squares.T, fisher_weight, preferred_element_type=jnp.float32)
            damping = DAMPING_SHARE * jnp.sum(fisher) / (FEATURES * CLASSES) + EPSILON
            denominator = fisher + damping
        change = gradient / denominator
        current = current - LEARNING_RATE * change
        moved = moved - change
        losses = is_valid * (row_peak + jnp.log(row_total) - label_logit)
    return moved, losses
```

```python
import functools

import jax
import jax.numpy as jnp
from jax import lax
from jax.experimental import pallas as pl
from jax.experimental.pallas import tpu as pltpu
from jax.sharding import PartitionSpec as P

ITERS = 2
NEGATIVE = -1e30
LEARNING_RATE = 2e-05
DAMPING_SHARE = 0.1
EPSILON = 1e-06
MESH = pl.DeviceIdType.MESH
UP, DOWN, SIDE, SIBLING = 0, 1, 2, 3
F32, BF16 = jnp.float32, jnp.bfloat16


def kernel(
    Z, Y, scale,
    features, weights, meta, active,
    moved, losses,
    x, xt, w, wlow, e_scr, r_scr, fw_scr, rec, g_scr,
    meta_all, stat1, stat2, damp_all, b_scr, ssq, loss_scr,
    own_sem, w_sem, gsend, grecv, wsend, wrecv, msend, mrecv,
    ssend, srecv, dsend, drecv, out_sem, osend, orecv,
):
    n = Z * Y
    nd = 2 * n
    rows_n = features.shape[0]
    half = features.shape[1]
    all_rows = n * rows_n
    ck = w.shape[2]
    me = lax.axis_index("example")
    k = lax.axis_index("cls")
    sib = 1 - k
    z, y = me // Y, lax.rem(me, Y)
    mine = me * 2 + k

    def rows(slot):
        return pl.ds(pl.multiple_of(slot * rows_n, rows_n), rows_n)

    def columns(index):
        return pl.ds(pl.multiple_of(index * ck, ck), ck)

    def remote(src, dst, ssem, rsem, example, core):
        return pltpu.make_async_remote_copy(
            src_ref=src, dst_ref=dst, send_sem=ssem, recv_sem=rsem,
            device_id={"example": example, "cls": core}, device_id_type=MESH,
        )

    own_copy = pltpu.make_async_copy(features, x.at[k, rows(me)], own_sem)
    own_copy.start()
    w_copy = pltpu.make_async_copy(weights.at[:, columns(k)], w.at[k], w_sem)
    w_copy.start()

    barrier = pltpu.get_barrier_semaphore()

    def greet(p, c):
        peer = lax.rem(mine + p, nd)
        pl.semaphore_signal(
            barrier, inc=1, device_id={"example": peer // 2, "cls": lax.rem(peer, 2)},
            device_id_type=MESH,
        )
        return c

    lax.fori_loop(1, nd, greet, 0)
    pl.semaphore_wait(barrier, nd - 1)

    def forward(slot, direction, src):
        target, core = {
            UP: (me + Y, k),
            DOWN: (me - Y, k),
            SIDE: (z * Y + (Y - 1 - y), k),
            SIBLING: (me, sib),
        }[direction]
        return remote(
            src, x.at[k, rows(slot)], gsend.at[direction, slot], grecv.at[k, slot], target, core
        )

    def landed(h, slot):
        remote(
            x.at[h, rows(slot)], x.at[h, rows(slot)], gsend.at[SIBLING, slot],
            grecv.at[h, slot], me, sib,
        ).wait_recv()

    meta_all[me] = meta[...]

    def meta_copy(p):
        peer = lax.rem(me + p, n)
        return peer, remote(
            meta, meta_all.at[me], msend.at[p], mrecv.at[me], peer, k
        )

    def meta_start(p, c):
        meta_copy(p)[1].start()
        return c

    def line(j, act, own=False):
        for sign in (1,) if own else (-1, 1):
            zz = z + sign * j
            slot = zz * Y + y
            src = features if own else x.at[k, rows(slot)]
            inside = jnp.logical_and(zz >= 0, zz < Z)

            @pl.when(inside)
            def _():
                act("enter", slot, None)
                if own or sign == -1:
                    @pl.when(z < Z - 1)
                    def _():
                        act("send", slot, forward(slot, UP, src))
                if own or sign == 1:
                    @pl.when(z > 0)
                    def _():
                        act("send", slot, forward(slot, DOWN, src))
                if Y == 2:
                    act("send", slot, forward(slot, SIDE, src))
                act("send", slot, forward(slot, SIBLING, src))

    def begin(kind, slot, copy):
        if kind == "enter":
            landed(k, slot)
        else:
            copy.start()

    def begin_own(kind, slot, copy):
        if kind == "send":
            copy.start()

    def finish(kind, slot, copy):
        if kind == "send":
            copy.wait_send()

    line(0, begin_own, own=True)
    lax.fori_loop(1, n, meta_start, 0)
    w_send = remote(weights.at[:, columns(sib)], w.at[k], wsend, wrecv, me, sib)
    w_send.start()

    def lower(h):
        step = min(512, half)

        def go(i, c):
            part = pl.ds(pl.multiple_of(i * step, step), step)
            wlow[h, part, :] = w[h, part, :].astype(BF16)
            return c

        lax.fori_loop(0, half // step, go, 0)

    w_copy.wait()
    lower(k)
    own_copy.wait()
    remote(w.at[sib], w.at[sib], wsend, wrecv, me, sib).wait_recv()
    lower(sib)

    def meta_wait(p, c):
        src = lax.rem(me + p, n)
        remote(meta, meta_all.at[src], msend.at[p], mrecv.at[src], me, sib).wait_recv()
        return c

    lax.fori_loop(1, n, meta_wait, 0)

    active_count = active[0]
    class_base = mine * ck
    class_index = class_base + lax.broadcasted_iota(jnp.int32, (rows_n, ck), 1)
    class_float = class_index.astype(F32)
    is_active = class_index < active_count
    lane = lax.broadcasted_iota(jnp.int32, (rows_n, rows_n), 1)

    def column(row):
        return jnp.broadcast_to(row, (rows_n, rows_n)).T[:, 0:1]

    def statistics(slot, logits, stat, with_label):
        masked = jnp.where(is_active, logits, NEGATIVE)
        peak = jnp.max(masked, axis=1, keepdims=True)
        exponent = jnp.exp(masked - peak)
        total = jnp.sum(exponent, axis=1, keepdims=True)
        e_scr[rows(slot), :] = exponent
        tile = jnp.where(lane == 0, peak, total)
        if with_label:
            target = column(meta_all[slot, 0:1, :])
            label = jnp.sum(
                jnp.where(class_float == target, logits, 0.0), axis=1, keepdims=True
            )
            tile = jnp.where(lane == 2, label, tile)
        tile = tile.T
        stat[mine, 0, pl.ds(slot, 1), :] = tile[0:1, :]
        stat[mine, 1, pl.ds(slot, 1), :] = tile[1:2, :]
        if with_label:
            stat[mine, 2, pl.ds(slot, 1), :] = tile[2:3, :]

    def process(slot):
        logits = None
        squares = None
        for h in range(2):
            block = x[h, rows(slot), :]
            xt[h, :, rows(slot)] = block.T
            term = jnp.sum((block * block).astype(F32), axis=1, keepdims=True)
            part = jnp.dot(block, wlow[h], preferred_element_type=F32)
            squares = term if h == 0 else squares + term
            logits = part if h == 0 else logits + part
        ssq[rows(slot), :] = jnp.broadcast_to(squares, (rows_n, 128))
        statistics(slot, logits, stat1, False)

    quarters = 2 * Y

    def gather(t, c):
        j, q = t // quarters, lax.rem(t, quarters)

        @pl.when(q == quarters - 2)
        def _():
            line(j + 1, begin)

        zz = z + (2 * lax.rem(q, 2) - 1) * j
        yy = y if Y == 1 else jnp.where(q < 2, y, 1 - y)
        slot = zz * Y + yy
        inside = jnp.logical_and(zz >= 0, zz < Z)
        inside = jnp.logical_and(inside, jnp.logical_or(j > 0, lax.rem(q, 2) == 1))

        @pl.when(inside)
        def _():
            if Y == 2:
                @pl.when(q >= 2)
                def _():
                    landed(k, slot)
                    forward(slot, SIBLING, x.at[k, rows(slot)]).start()

            landed(sib, slot)
            process(slot)

        return c

    lax.fori_loop(0, Z * quarters, gather, 0)

    def share(buffer, count, ssem, rsem):
        def piece(slot):
            return buffer.at[slot] if count is None else buffer.at[slot, pl.ds(0, count)]

        def copy(p):
            peer = lax.rem(mine + p, nd)
            return remote(
                piece(mine), piece(mine), ssem.at[p], rsem.at[mine], peer // 2, lax.rem(peer, 2)
            )

        def start(p, c):
            copy(p).start()
            return c

        def wait_in(p, c):
            src = lax.rem(mine + p, nd)
            remote(
                piece(src), piece(src), ssem.at[p], rsem.at[src], me, sib
            ).wait_recv()
            return c

        def wait_out(p, c):
            copy(p).wait_send()
            return c

        return (
            lambda: lax.fori_loop(1, nd, start, 0),
            lambda: lax.fori_loop(1, nd, wait_in, 0),
            lambda: lax.fori_loop(1, nd, wait_out, 0),
        )

    counts = meta_all[:, 1, :]
    valid_total = jnp.sum(counts[:, 0:1], axis=0, keepdims=True)

    def combine(stat):
        peak = stat[0, 0]
        for d in range(1, nd):
            peak = jnp.maximum(peak, stat[d, 0])
        total = jnp.zeros_like(peak)
        for d in range(nd):
            total = total + stat[d, 1] * jnp.exp(stat[d, 0] - peak)
        b_scr[...] = jnp.exp(stat[mine, 0] - peak) / total
        return peak, total

    row_number = lax.broadcasted_iota(jnp.int32, (rows_n, 1), 0).astype(F32)

    def residuals(first):
        def go(i, acc):
            valid = (row_number < meta_all[i, 1:2, 0:1]).astype(F32) / valid_total
            target = column(meta_all[i, 0:1, :])
            probability = e_scr[rows(i), :] * column(b_scr[pl.ds(i, 1), :])
            is_label = (class_float == target).astype(F32)
            r_scr[rows(i), :] = (valid * (probability - is_label)).astype(BF16)
            if first:
                fw = (valid * probability * (1.0 - probability)).astype(BF16)
                fw_scr[rows(i), :] = fw
                row_sum = jnp.sum(fw.astype(F32), axis=1, keepdims=True)
                acc = acc + jnp.sum(row_sum * ssq[rows(i), 0:1], axis=0, keepdims=True)
            return acc

        return lax.fori_loop(0, n, go, jnp.zeros((1, 1), F32))

    start1, in1, out1 = share(stat1, None, ssend.at[0], srecv.at[0])
    start1()
    in1()
    combine(stat1)
    fisher_part = residuals(True)
    damp_all[mine] = jnp.broadcast_to(fisher_part, damp_all.shape[1:])
    start_d, in_d, out_d = share(damp_all, None, dsend, drecv)
    start_d()

    step = min(512, half)
    per_half = half // step

    def chunk(i):
        return i // per_half, pl.ds(pl.multiple_of(lax.rem(i, per_half) * step, step), step)

    def gradient(i, c):
        h, part = chunk(i)
        g_scr[h, part, :] = jnp.dot(xt[h, part, :], r_scr[...], preferred_element_type=F32)
        return c

    lax.fori_loop(0, 2 * per_half, gradient, 0)

    in_d()
    fisher_sum = damp_all[0, 0:1, 0:1]
    for d in range(1, nd):
        fisher_sum = fisher_sum + damp_all[d, 0:1, 0:1]
    damping = DAMPING_SHARE * fisher_sum / scale + EPSILON
    e_scr[...] = jnp.zeros_like(e_scr)

    def fisher_step(i, c):
        h, part = chunk(i)
        block = xt[h, part, :]
        fisher = jnp.dot(block * block, fw_scr[...], preferred_element_type=F32)
        inverse = 1.0 / (fisher + damping)
        rec[h, part, :] = inverse
        change = g_scr[h, part, :] * inverse
        g_scr[h, part, :] = change
        low = (w[h, part, :] - LEARNING_RATE * change).astype(BF16)
        wlow[h, part, :] = low
        e_scr[...] += jnp.dot(x[h, :, part], low, preferred_element_type=F32)
        return c

    lax.fori_loop(0, 2 * per_half, fisher_step, 0)

    def second(i, c):
        statistics(i, e_scr[rows(i), :], stat2, True)
        return c

    lax.fori_loop(0, n, second, 0)
    start2, in2, out2 = share(stat2, None, ssend.at[1], srecv.at[1])
    start2()
    in2()
    peak, total = combine(stat2)
    label = stat2[0, 2]
    for d in range(1, nd):
        label = label + stat2[d, 2]
    lane_row = lax.broadcasted_iota(jnp.int32, (n, rows_n), 1).astype(F32)
    loss_scr[...] = (lane_row < counts).astype(F32) * (peak + jnp.log(total) - label)
    losses[...] = loss_scr[pl.ds(me, 1), :]
    residuals(False)

    def place(i):
        h = jnp.where(i < per_half, sib, k)
        return h, pl.ds(pl.multiple_of(lax.rem(i, per_half) * step, step), step)

    def out_remote(i):
        h, part = place(i)
        return remote(
            w.at[h, part, :], moved.at[part, columns(k)], osend.at[i], orecv.at[i], me, sib
        )

    def out_local(i):
        h, part = place(i)
        return pltpu.make_async_copy(
            w.at[h, part, :], moved.at[part, columns(k)], out_sem.at[i - per_half]
        )

    def last(i, c):
        h, part = place(i)
        grad = jnp.dot(xt[h, part, :], r_scr[...], preferred_element_type=F32)
        w[h, part, :] = -g_scr[h, part, :] - grad * rec[h, part, :]

        @pl.when(i < per_half)
        def _():
            out_remote(i).start()

        @pl.when(i >= per_half)
        def _():
            out_local(i).start()

        return c

    w_send.wait_send()
    lax.fori_loop(0, 2 * per_half, last, 0)

    line(0, finish, own=True)

    def drain(j, c):
        line(j, finish)
        return c

    lax.fori_loop(1, Z, drain, 0)
    if Y == 2:
        def drain_side(zz, c):
            slot = zz * Y + (1 - y)
            forward(slot, SIBLING, x.at[k, rows(slot)]).wait_send()
            return c

        lax.fori_loop(0, Z, drain_side, 0)

    def meta_done(p, c):
        meta_copy(p)[1].wait_send()
        return c

    lax.fori_loop(1, n, meta_done, 0)
    out1()
    out_d()
    out2()

    def out_done(i, c):
        out_remote(i).wait_send()
        _, part = place(i)
        remote(
            w.at[k, part, :], moved.at[part, columns(sib)], osend.at[i], orecv.at[i], me, sib
        ).wait_recv()
        out_local(i + per_half).wait()
        return c

    lax.fori_loop(0, per_half, out_done, 0)


def solution(mesh):
    n = mesh.shape["example"]
    Y = 2 if n == 8 else 1
    Z = n // Y
    nd = 2 * n

    def body(features, weights, labels, counts, active):
        rows_n, half = features.shape
        local = weights.shape[1]
        ck = local // 2
        all_rows = rows_n * n
        target = (labels % active[0]).astype(F32)
        meta = jnp.concatenate(
            [
                target[None, :],
                jnp.broadcast_to(counts.astype(F32)[:, None], (7, rows_n)),
            ],
            axis=0,
        )
        scale = float(half * 2 * local * n)
        per_half = half // min(512, half)
        dma = pltpu.SemaphoreType.DMA
        moved, losses = pl.pallas_call(
            functools.partial(kernel, Z, Y, scale),
            out_shape=(
                jax.ShapeDtypeStruct(weights.shape, F32),
                jax.ShapeDtypeStruct((1, rows_n), F32),
            ),
            in_specs=[
                pl.BlockSpec(memory_space=pl.ANY),
                pl.BlockSpec(memory_space=pl.ANY),
                pl.BlockSpec(memory_space=pltpu.VMEM),
                pl.BlockSpec(memory_space=pltpu.SMEM),
            ],
            out_specs=(
                pl.BlockSpec(memory_space=pl.ANY),
                pl.BlockSpec(memory_space=pltpu.VMEM),
            ),
            scratch_shapes=[
                pltpu.VMEM((2, all_rows, half), BF16),
                pltpu.VMEM((2, half, all_rows), BF16),
                pltpu.VMEM((2, half, ck), F32),
                pltpu.VMEM((2, half, ck), BF16),
                pltpu.VMEM((all_rows, ck), F32),
                pltpu.VMEM((all_rows, ck), BF16),
                pltpu.VMEM((all_rows, ck), BF16),
                pltpu.VMEM((2, half, ck), F32),
                pltpu.VMEM((2, half, ck), F32),
                pltpu.VMEM((n, 8, rows_n), F32),
                pltpu.VMEM((nd, 2, n, rows_n), F32),
                pltpu.VMEM((nd, 3, n, rows_n), F32),
                pltpu.VMEM((nd, 8, 128), F32),
                pltpu.VMEM((n, rows_n), F32),
                pltpu.VMEM((all_rows, 128), F32),
                pltpu.VMEM((n, rows_n), F32),
                dma, dma,
                dma((4, n)), dma((2, n)),
                dma, dma,
                dma((n,)), dma((n,)),
                dma((2, nd)), dma((2, nd)),
                dma((nd,)), dma((nd,)),
                dma((per_half,)), dma((per_half,)), dma((per_half,)),
            ],
            compiler_params=pltpu.CompilerParams(
                collective_id=0, has_side_effects=True, vmem_limit_bytes=67043328
            ),
        )(features, weights, meta, active)
        return moved, losses.reshape(rows_n)

    return jax.shard_map(
        body,
        mesh=mesh,
        in_specs=(
            P(("groups", "example"), "cls"),
            P(("groups", "cls"), "example"),
            P(("groups", "example")),
            P(("groups", "example")),
            P("groups"),
        ),
        out_specs=(P(("groups", "cls"), "example"), P(("groups", "example"))),
        check_vma=False,
    )
```

```python
import functools

import jax
import jax.numpy as jnp
from jax import lax
from jax.experimental import pallas as pl
from jax.experimental.pallas import tpu as pltpu
from jax.sharding import PartitionSpec as P

ITERS = 2
NEGATIVE = -1e30
LEARNING_RATE = 2e-05
DAMPING_SHARE = 0.1
EPSILON = 1e-06
MESH = pl.DeviceIdType.MESH
UP, DOWN, SIDE, SIBLING = 0, 1, 2, 3
F32, BF16 = jnp.float32, jnp.bfloat16


def kernel(
    Z, Y, scale,
    features, weights, meta, active,
    moved, losses,
    x, xt, w, wlow, e_scr, r_scr, fw_scr, rec, g_scr,
    meta_all, stat1, stat2, damp_all, b_scr, ssq, loss_scr,
    own_sem, w_sem, gsend, grecv, wsend, wrecv, msend, mrecv,
    ssend, srecv, dsend, drecv, out_sem, osend, orecv,
):
    n = Z * Y
    nd = 2 * n
    rows_n = features.shape[0]
    half = features.shape[1]
    all_rows = n * rows_n
    ck = w.shape[2]
    me = lax.axis_index("example")
    k = lax.axis_index("cls")
    sib = 1 - k
    z, y = me // Y, lax.rem(me, Y)
    is_end = jnp.logical_or(z == 0, z == Z - 1)
    mine = me * 2 + k

    def rows(slot):
        return pl.ds(pl.multiple_of(slot * rows_n, rows_n), rows_n)

    def columns(index):
        return pl.ds(pl.multiple_of(index * ck, ck), ck)

    def remote(src, dst, ssem, rsem, example, core):
        return pltpu.make_async_remote_copy(
            src_ref=src, dst_ref=dst, send_sem=ssem, recv_sem=rsem,
            device_id={"example": example, "cls": core}, device_id_type=MESH,
        )

    own_copy = pltpu.make_async_copy(features, x.at[k, rows(me)], own_sem)
    own_copy.start()
    w_copy = pltpu.make_async_copy(weights.at[:, columns(k)], w.at[k], w_sem)
    w_copy.start()

    barrier = pltpu.get_barrier_semaphore()

    def greet(p, c):
        peer = lax.rem(mine + p, nd)
        pl.semaphore_signal(
            barrier, inc=1, device_id={"example": peer // 2, "cls": lax.rem(peer, 2)},
            device_id_type=MESH,
        )
        return c

    lax.fori_loop(1, nd, greet, 0)
    pl.semaphore_wait(barrier, nd - 1)

    def forward(slot, direction, src, second=None):
        place = rows(slot)
        if second is not None:
            size = rows_n // 2
            place = pl.ds(pl.multiple_of(slot * rows_n + second * size, size), size)
            src = x.at[k, place]
        target, core = {
            UP: (me + Y, k),
            DOWN: (me - Y, k),
            SIDE: (z * Y + (Y - 1 - y), k),
            SIBLING: (me, sib),
        }[direction]
        return remote(
            src, x.at[k, place], gsend.at[direction, slot], grecv.at[k, slot], target, core
        )

    def landed(h, slot):
        remote(
            x.at[h, rows(slot)], x.at[h, rows(slot)], gsend.at[SIBLING, slot],
            grecv.at[h, slot], me, sib,
        ).wait_recv()

    meta_all[me] = meta[...]

    def meta_copy(p):
        peer = lax.rem(me + p, n)
        return peer, remote(
            meta, meta_all.at[me], msend.at[p], mrecv.at[me], peer, k
        )

    def meta_start(p, c):
        meta_copy(p)[1].start()
        return c

    def line(j, act, own=False):
        for sign in (1,) if own else (-1, 1):
            zz = z + sign * j
            slot = zz * Y + y
            src = features if own else x.at[k, rows(slot)]
            inside = jnp.logical_and(zz >= 0, zz < Z)

            @pl.when(inside)
            def _():
                act("enter", slot, None)
                if own or sign == -1:
                    @pl.when(z < Z - 1)
                    def _():
                        act("send", slot, forward(slot, UP, src))
                if own or sign == 1:
                    @pl.when(z > 0)
                    def _():
                        act("send", slot, forward(slot, DOWN, src))
                if Y == 2 and own:
                    act("send", slot, forward(slot, SIDE, src))
                elif Y == 2:
                    far = jnp.logical_and(is_end, j == Z - 1)
                    edge = jnp.logical_or(zz == 0, zz == Z - 1)
                    near = jnp.logical_and(jnp.logical_not(is_end), edge)
                    near = jnp.logical_and(near, j == 1)

                    @pl.when(far)
                    def _():
                        act("send", slot, forward(slot, SIDE, src, 0))

                    @pl.when(jnp.logical_not(jnp.logical_or(far, near)))
                    def _():
                        act("send", slot, forward(slot, SIDE, src))
                act("send", slot, forward(slot, SIBLING, src))

    def cross(j, slot, act):
        src = x.at[k, rows(slot)]

        @pl.when(jnp.logical_and(z == 0, j == 0))
        def _():
            act(forward(slot, UP, src))

        @pl.when(jnp.logical_and(z == Z - 1, j == 0))
        def _():
            act(forward(slot, DOWN, src))

        @pl.when(jnp.logical_and(z == 1, j == 2))
        def _():
            act(forward(slot, DOWN, src, 1))

        @pl.when(jnp.logical_and(z == 2, j == 2))
        def _():
            act(forward(slot, UP, src, 1))

        act(forward(slot, SIBLING, src))

    def begin(kind, slot, copy):
        if kind == "enter":
            landed(k, slot)
        else:
            copy.start()

    def begin_own(kind, slot, copy):
        if kind == "send":
            copy.start()

    def finish(kind, slot, copy):
        if kind == "send":
            copy.wait_send()

    line(0, begin_own, own=True)
    lax.fori_loop(1, n, meta_start, 0)
    w_send = remote(weights.at[:, columns(sib)], w.at[k], wsend, wrecv, me, sib)
    w_send.start()

    def lower(h):
        step = min(512, half)

        def go(i, c):
            part = pl.ds(pl.multiple_of(i * step, step), step)
            wlow[h, part, :] = w[h, part, :].astype(BF16)
            return c

        lax.fori_loop(0, half // step, go, 0)

    w_copy.wait()
    lower(k)
    own_copy.wait()
    remote(w.at[sib], w.at[sib], wsend, wrecv, me, sib).wait_recv()
    lower(sib)

    def meta_wait(p, c):
        src = lax.rem(me + p, n)
        remote(meta, meta_all.at[src], msend.at[p], mrecv.at[src], me, sib).wait_recv()
        return c

    lax.fori_loop(1, n, meta_wait, 0)

    active_count = active[0]
    class_base = mine * ck
    class_index = class_base + lax.broadcasted_iota(jnp.int32, (rows_n, ck), 1)
    class_float = class_index.astype(F32)
    is_active = class_index < active_count
    lane = lax.broadcasted_iota(jnp.int32, (rows_n, rows_n), 1)

    def column(row):
        return jnp.broadcast_to(row, (rows_n, rows_n)).T[:, 0:1]

    def statistics(slot, logits, stat, with_label):
        masked = jnp.where(is_active, logits, NEGATIVE)
        peak = jnp.max(masked, axis=1, keepdims=True)
        exponent = jnp.exp(masked - peak)
        total = jnp.sum(exponent, axis=1, keepdims=True)
        e_scr[rows(slot), :] = exponent
        tile = jnp.where(lane == 0, peak, total)
        if with_label:
            target = column(meta_all[slot, 0:1, :])
            label = jnp.sum(
                jnp.where(class_float == target, logits, 0.0), axis=1, keepdims=True
            )
            tile = jnp.where(lane == 2, label, tile)
        tile = tile.T
        stat[mine, 0, pl.ds(slot, 1), :] = tile[0:1, :]
        stat[mine, 1, pl.ds(slot, 1), :] = tile[1:2, :]
        if with_label:
            stat[mine, 2, pl.ds(slot, 1), :] = tile[2:3, :]

    def process(slot):
        logits = None
        squares = None
        for h in range(2):
            block = x[h, rows(slot), :]
            xt[h, :, rows(slot)] = block.T
            term = jnp.sum((block * block).astype(F32), axis=1, keepdims=True)
            part = jnp.dot(block, wlow[h], preferred_element_type=F32)
            squares = term if h == 0 else squares + term
            logits = part if h == 0 else logits + part
        ssq[rows(slot), :] = jnp.broadcast_to(squares, (rows_n, 128))
        statistics(slot, logits, stat1, False)

    quarters = 2 * Y

    def gather(t, c):
        j, q = t // quarters, lax.rem(t, quarters)

        @pl.when(q == quarters - 2)
        def _():
            line(j + 1, begin)

        zz = z + (2 * lax.rem(q, 2) - 1) * j
        yy = y if Y == 1 else jnp.where(q < 2, y, 1 - y)
        slot = zz * Y + yy
        inside = jnp.logical_and(zz >= 0, zz < Z)
        inside = jnp.logical_and(inside, jnp.logical_or(j > 0, lax.rem(q, 2) == 1))

        @pl.when(inside)
        def _():
            if Y == 2:
                @pl.when(q >= 2)
                def _():
                    landed(k, slot)
                    cross(j, slot, lambda copy: copy.start())

            landed(sib, slot)
            process(slot)

        return c

    lax.fori_loop(0, Z * quarters, gather, 0)

    def share(buffer, count, ssem, rsem):
        def piece(slot):
            return buffer.at[slot] if count is None else buffer.at[slot, pl.ds(0, count)]

        def copy(p):
            peer = lax.rem(mine + p, nd)
            return remote(
                piece(mine), piece(mine), ssem.at[p], rsem.at[mine], peer // 2, lax.rem(peer, 2)
            )

        def start(p, c):
            copy(p).start()
            return c

        def wait_in(p, c):
            src = lax.rem(mine + p, nd)
            remote(
                piece(src), piece(src), ssem.at[p], rsem.at[src], me, sib
            ).wait_recv()
            return c

        def wait_out(p, c):
            copy(p).wait_send()
            return c

        return (
            lambda: lax.fori_loop(1, nd, start, 0),
            lambda: lax.fori_loop(1, nd, wait_in, 0),
            lambda: lax.fori_loop(1, nd, wait_out, 0),
        )

    counts = meta_all[:, 1, :]
    valid_total = jnp.sum(counts[:, 0:1], axis=0, keepdims=True)

    def combine(stat):
        peak = stat[0, 0]
        for d in range(1, nd):
            peak = jnp.maximum(peak, stat[d, 0])
        total = jnp.zeros_like(peak)
        for d in range(nd):
            total = total + stat[d, 1] * jnp.exp(stat[d, 0] - peak)
        b_scr[...] = jnp.exp(stat[mine, 0] - peak) / total
        return peak, total

    row_number = lax.broadcasted_iota(jnp.int32, (rows_n, 1), 0).astype(F32)

    def residuals(first):
        def go(i, acc):
            valid = (row_number < meta_all[i, 1:2, 0:1]).astype(F32) / valid_total
            target = column(meta_all[i, 0:1, :])
            probability = e_scr[rows(i), :] * column(b_scr[pl.ds(i, 1), :])
            is_label = (class_float == target).astype(F32)
            r_scr[rows(i), :] = (valid * (probability - is_label)).astype(BF16)
            if first:
                fw = (valid * probability * (1.0 - probability)).astype(BF16)
                fw_scr[rows(i), :] = fw
                row_sum = jnp.sum(fw.astype(F32), axis=1, keepdims=True)
                acc = acc + jnp.sum(row_sum * ssq[rows(i), 0:1], axis=0, keepdims=True)
            return acc

        return lax.fori_loop(0, n, go, jnp.zeros((1, 1), F32))

    start1, in1, out1 = share(stat1, None, ssend.at[0], srecv.at[0])
    start1()
    in1()
    combine(stat1)
    fisher_part = residuals(True)
    damp_all[mine] = jnp.broadcast_to(fisher_part, damp_all.shape[1:])
    start_d, in_d, out_d = share(damp_all, None, dsend, drecv)
    start_d()

    step = min(512, half)
    per_half = half // step

    def chunk(i):
        return i // per_half, pl.ds(pl.multiple_of(lax.rem(i, per_half) * step, step), step)

    def gradient(i, c):
        h, part = chunk(i)
        g_scr[h, part, :] = jnp.dot(xt[h, part, :], r_scr[...], preferred_element_type=F32)
        return c

    lax.fori_loop(0, 2 * per_half, gradient, 0)

    in_d()
    fisher_sum = damp_all[0, 0:1, 0:1]
    for d in range(1, nd):
        fisher_sum = fisher_sum + damp_all[d, 0:1, 0:1]
    damping = DAMPING_SHARE * fisher_sum / scale + EPSILON
    e_scr[...] = jnp.zeros_like(e_scr)

    def fisher_step(i, c):
        h, part = chunk(i)
        block = xt[h, part, :]
        fisher = jnp.dot(block * block, fw_scr[...], preferred_element_type=F32)
        inverse = 1.0 / (fisher + damping)
        rec[h, part, :] = inverse
        change = g_scr[h, part, :] * inverse
        g_scr[h, part, :] = change
        low = (w[h, part, :] - LEARNING_RATE * change).astype(BF16)
        wlow[h, part, :] = low
        e_scr[...] += jnp.dot(x[h, :, part], low, preferred_element_type=F32)
        return c

    lax.fori_loop(0, 2 * per_half, fisher_step, 0)

    def second(i, c):
        statistics(i, e_scr[rows(i), :], stat2, True)
        return c

    lax.fori_loop(0, n, second, 0)
    start2, in2, out2 = share(stat2, None, ssend.at[1], srecv.at[1])
    start2()
    in2()
    peak, total = combine(stat2)
    label = stat2[0, 2]
    for d in range(1, nd):
        label = label + stat2[d, 2]
    lane_row = lax.broadcasted_iota(jnp.int32, (n, rows_n), 1).astype(F32)
    loss_scr[...] = (lane_row < counts).astype(F32) * (peak + jnp.log(total) - label)
    losses[...] = loss_scr[pl.ds(me, 1), :]
    residuals(False)

    def place(i):
        h = jnp.where(i < per_half, sib, k)
        return h, pl.ds(pl.multiple_of(lax.rem(i, per_half) * step, step), step)

    def out_remote(i):
        h, part = place(i)
        return remote(
            w.at[h, part, :], moved.at[part, columns(k)], osend.at[i], orecv.at[i], me, sib
        )

    def out_local(i):
        h, part = place(i)
        return pltpu.make_async_copy(
            w.at[h, part, :], moved.at[part, columns(k)], out_sem.at[i - per_half]
        )

    def last(i, c):
        h, part = place(i)
        grad = jnp.dot(xt[h, part, :], r_scr[...], preferred_element_type=F32)
        w[h, part, :] = -g_scr[h, part, :] - grad * rec[h, part, :]

        @pl.when(i < per_half)
        def _():
            out_remote(i).start()

        @pl.when(i >= per_half)
        def _():
            out_local(i).start()

        return c

    w_send.wait_send()
    lax.fori_loop(0, 2 * per_half, last, 0)

    line(0, finish, own=True)

    def drain(j, c):
        line(j, finish)
        return c

    lax.fori_loop(1, Z, drain, 0)
    if Y == 2:
        def drain_side(zz, c):
            slot = zz * Y + (1 - y)
            cross(jnp.abs(zz - z), slot, lambda copy: copy.wait_send())
            return c

        lax.fori_loop(0, Z, drain_side, 0)

    def meta_done(p, c):
        meta_copy(p)[1].wait_send()
        return c

    lax.fori_loop(1, n, meta_done, 0)
    out1()
    out_d()
    out2()

    def out_done(i, c):
        out_remote(i).wait_send()
        _, part = place(i)
        remote(
            w.at[k, part, :], moved.at[part, columns(sib)], osend.at[i], orecv.at[i], me, sib
        ).wait_recv()
        out_local(i + per_half).wait()
        return c

    lax.fori_loop(0, per_half, out_done, 0)


def solution(mesh):
    n = mesh.shape["example"]
    Y = 2 if n == 8 else 1
    Z = n // Y
    nd = 2 * n

    def body(features, weights, labels, counts, active):
        rows_n, half = features.shape
        local = weights.shape[1]
        ck = local // 2
        all_rows = rows_n * n
        target = (labels % active[0]).astype(F32)
        meta = jnp.concatenate(
            [
                target[None, :],
                jnp.broadcast_to(counts.astype(F32)[:, None], (7, rows_n)),
            ],
            axis=0,
        )
        scale = float(half * 2 * local * n)
        per_half = half // min(512, half)
        dma = pltpu.SemaphoreType.DMA
        moved, losses = pl.pallas_call(
            functools.partial(kernel, Z, Y, scale),
            out_shape=(
                jax.ShapeDtypeStruct(weights.shape, F32),
                jax.ShapeDtypeStruct((1, rows_n), F32),
            ),
            in_specs=[
                pl.BlockSpec(memory_space=pl.ANY),
                pl.BlockSpec(memory_space=pl.ANY),
                pl.BlockSpec(memory_space=pltpu.VMEM),
                pl.BlockSpec(memory_space=pltpu.SMEM),
            ],
            out_specs=(
                pl.BlockSpec(memory_space=pl.ANY),
                pl.BlockSpec(memory_space=pltpu.VMEM),
            ),
            scratch_shapes=[
                pltpu.VMEM((2, all_rows, half), BF16),
                pltpu.VMEM((2, half, all_rows), BF16),
                pltpu.VMEM((2, half, ck), F32),
                pltpu.VMEM((2, half, ck), BF16),
                pltpu.VMEM((all_rows, ck), F32),
                pltpu.VMEM((all_rows, ck), BF16),
                pltpu.VMEM((all_rows, ck), BF16),
                pltpu.VMEM((2, half, ck), F32),
                pltpu.VMEM((2, half, ck), F32),
                pltpu.VMEM((n, 8, rows_n), F32),
                pltpu.VMEM((nd, 2, n, rows_n), F32),
                pltpu.VMEM((nd, 3, n, rows_n), F32),
                pltpu.VMEM((nd, 8, 128), F32),
                pltpu.VMEM((n, rows_n), F32),
                pltpu.VMEM((all_rows, 128), F32),
                pltpu.VMEM((n, rows_n), F32),
                dma, dma,
                dma((4, n)), dma((2, n)),
                dma, dma,
                dma((n,)), dma((n,)),
                dma((2, nd)), dma((2, nd)),
                dma((nd,)), dma((nd,)),
                dma((per_half,)), dma((per_half,)), dma((per_half,)),
            ],
            compiler_params=pltpu.CompilerParams(
                collective_id=0, has_side_effects=True, vmem_limit_bytes=67043328
            ),
        )(features, weights, meta, active)
        return moved, losses.reshape(rows_n)

    return jax.shard_map(
        body,
        mesh=mesh,
        in_specs=(
            P(("groups", "example"), "cls"),
            P(("groups", "cls"), "example"),
            P(("groups", "example")),
            P(("groups", "example")),
            P("groups"),
        ),
        out_specs=(P(("groups", "cls"), "example"), P(("groups", "example"))),
        check_vma=False,
    )
```

```python
import functools

import jax
import jax.numpy as jnp
from jax import lax
from jax.experimental import pallas as pl
from jax.experimental.pallas import tpu as pltpu
from jax.sharding import PartitionSpec as P

ITERS = 2
NEGATIVE = -1e30
LEARNING_RATE = 2e-05
DAMPING_SHARE = 0.1
EPSILON = 1e-06
MESH = pl.DeviceIdType.MESH
UP, DOWN, SIDE, SIBLING = 0, 1, 2, 3
F32, BF16 = jnp.float32, jnp.bfloat16


def kernel(
    Z, Y, scale,
    features, weights, meta, active,
    moved, losses,
    x, xt, w, wlow, e_scr, r_scr, fw_scr, rec, g_scr,
    meta_all, stat1, stat2, damp_all, b_scr, ssq, loss_scr,
    own_sem, w_sem, gsend, grecv, wsend, wrecv, msend, mrecv,
    ssend, srecv, dsend, drecv, out_sem, osend, orecv,
):
    n = Z * Y
    nd = 2 * n
    rows_n = features.shape[0]
    half = features.shape[1]
    all_rows = n * rows_n
    ck = w.shape[2]
    me = lax.axis_index("example")
    k = lax.axis_index("cls")
    sib = 1 - k
    z, y = me // Y, lax.rem(me, Y)
    is_end = jnp.logical_or(z == 0, z == Z - 1)
    mine = me * 2 + k

    def rows(slot):
        return pl.ds(pl.multiple_of(slot * rows_n, rows_n), rows_n)

    def columns(index):
        return pl.ds(pl.multiple_of(index * ck, ck), ck)

    def remote(src, dst, ssem, rsem, example, core):
        return pltpu.make_async_remote_copy(
            src_ref=src, dst_ref=dst, send_sem=ssem, recv_sem=rsem,
            device_id={"example": example, "cls": core}, device_id_type=MESH,
        )

    own_copy = pltpu.make_async_copy(features, x.at[k, rows(me)], own_sem)
    own_copy.start()
    w_copy = pltpu.make_async_copy(weights.at[:, columns(k)], w.at[k], w_sem)
    w_copy.start()

    barrier = pltpu.get_barrier_semaphore()

    def greet(example, core):
        pl.semaphore_signal(
            barrier, inc=1, device_id={"example": example, "cls": core}, device_id_type=MESH
        )

    greet(me, sib)
    if Y == 2:
        greet(z * Y + (1 - y), k)

    @pl.when(z < Z - 1)
    def _():
        greet(me + Y, k)

    @pl.when(z > 0)
    def _():
        greet(me - Y, k)

    pl.semaphore_wait(barrier, Y + (z < Z - 1).astype(jnp.int32) + (z > 0).astype(jnp.int32))

    def forward(slot, direction, src, second=None):
        place = rows(slot)
        if second is not None:
            size = rows_n // 2
            place = pl.ds(pl.multiple_of(slot * rows_n + second * size, size), size)
            src = x.at[k, place]
        target, core = {
            UP: (me + Y, k),
            DOWN: (me - Y, k),
            SIDE: (z * Y + (Y - 1 - y), k),
            SIBLING: (me, sib),
        }[direction]
        return remote(
            src, x.at[k, place], gsend.at[direction, slot], grecv.at[k, slot], target, core
        )

    def landed(h, slot):
        remote(
            x.at[h, rows(slot)], x.at[h, rows(slot)], gsend.at[SIBLING, slot],
            grecv.at[h, slot], me, sib,
        ).wait_recv()

    meta_all[me] = meta[...]

    def meta_copy(p):
        peer = lax.rem(me + p, n)
        return peer, remote(
            meta, meta_all.at[me], msend.at[p], mrecv.at[me], peer, k
        )

    def meta_start(p, c):
        meta_copy(p)[1].start()
        return c

    def line(j, act, own=False):
        for sign in (1,) if own else (-1, 1):
            zz = z + sign * j
            slot = zz * Y + y
            src = features if own else x.at[k, rows(slot)]
            inside = jnp.logical_and(zz >= 0, zz < Z)

            @pl.when(inside)
            def _():
                act("enter", slot, None)
                if own or sign == -1:
                    @pl.when(z < Z - 1)
                    def _():
                        act("send", slot, forward(slot, UP, src))
                if own or sign == 1:
                    @pl.when(z > 0)
                    def _():
                        act("send", slot, forward(slot, DOWN, src))
                if Y == 2 and own:
                    act("send", slot, forward(slot, SIDE, src))
                elif Y == 2:
                    far = jnp.logical_and(is_end, j == Z - 1)
                    edge = jnp.logical_or(zz == 0, zz == Z - 1)
                    near = jnp.logical_and(jnp.logical_not(is_end), edge)
                    near = jnp.logical_and(near, j == 1)

                    @pl.when(far)
                    def _():
                        act("send", slot, forward(slot, SIDE, src, 0))

                    @pl.when(jnp.logical_not(jnp.logical_or(far, near)))
                    def _():
                        act("send", slot, forward(slot, SIDE, src))
                act("send", slot, forward(slot, SIBLING, src))

    def cross(j, slot, act):
        src = x.at[k, rows(slot)]

        @pl.when(jnp.logical_and(z == 0, j == 0))
        def _():
            act(forward(slot, UP, src))

        @pl.when(jnp.logical_and(z == Z - 1, j == 0))
        def _():
            act(forward(slot, DOWN, src))

        @pl.when(jnp.logical_and(z == 1, j == 2))
        def _():
            act(forward(slot, DOWN, src, 1))

        @pl.when(jnp.logical_and(z == 2, j == 2))
        def _():
            act(forward(slot, UP, src, 1))

        act(forward(slot, SIBLING, src))

    def begin(kind, slot, copy):
        if kind == "enter":
            landed(k, slot)
        else:
            copy.start()

    def begin_own(kind, slot, copy):
        if kind == "send":
            copy.start()

    def finish(kind, slot, copy):
        if kind == "send":
            copy.wait_send()

    line(0, begin_own, own=True)
    w_send = remote(weights.at[:, columns(sib)], w.at[k], wsend, wrecv, me, sib)
    w_send.start()

    def lower(h):
        step = min(512, half)

        def go(i, c):
            part = pl.ds(pl.multiple_of(i * step, step), step)
            wlow[h, part, :] = w[h, part, :].astype(BF16)
            return c

        lax.fori_loop(0, half // step, go, 0)

    w_copy.wait()
    lower(k)
    own_copy.wait()
    remote(w.at[sib], w.at[sib], wsend, wrecv, me, sib).wait_recv()
    lower(sib)

    def meta_wait(p, c):
        src = lax.rem(me + p, n)
        remote(meta, meta_all.at[src], msend.at[p], mrecv.at[src], me, sib).wait_recv()
        return c


    active_count = active[0]
    class_base = mine * ck
    class_index = class_base + lax.broadcasted_iota(jnp.int32, (rows_n, ck), 1)
    class_float = class_index.astype(F32)
    is_active = class_index < active_count
    lane = lax.broadcasted_iota(jnp.int32, (rows_n, rows_n), 1)

    def column(row):
        return jnp.broadcast_to(row, (rows_n, rows_n)).T[:, 0:1]

    def statistics(slot, logits, stat, with_label):
        masked = jnp.where(is_active, logits, NEGATIVE)
        peak = jnp.max(masked, axis=1, keepdims=True)
        exponent = jnp.exp(masked - peak)
        total = jnp.sum(exponent, axis=1, keepdims=True)
        e_scr[rows(slot), :] = exponent
        tile = jnp.where(lane == 0, peak, total)
        if with_label:
            target = column(meta_all[slot, 0:1, :])
            label = jnp.sum(
                jnp.where(class_float == target, logits, 0.0), axis=1, keepdims=True
            )
            tile = jnp.where(lane == 2, label, tile)
        tile = tile.T
        stat[mine, 0, pl.ds(slot, 1), :] = tile[0:1, :]
        stat[mine, 1, pl.ds(slot, 1), :] = tile[1:2, :]
        if with_label:
            stat[mine, 2, pl.ds(slot, 1), :] = tile[2:3, :]

    def process(slot):
        logits = None
        squares = None
        for h in range(2):
            block = x[h, rows(slot), :]
            xt[h, :, rows(slot)] = block.T
            term = jnp.sum((block * block).astype(F32), axis=1, keepdims=True)
            part = jnp.dot(block, wlow[h], preferred_element_type=F32)
            squares = term if h == 0 else squares + term
            logits = part if h == 0 else logits + part
        ssq[rows(slot), :] = jnp.broadcast_to(squares, (rows_n, 128))
        statistics(slot, logits, stat1, False)

    quarters = 2 * Y

    def gather(t, c):
        j, q = t // quarters, lax.rem(t, quarters)

        @pl.when(q == quarters - 2)
        def _():
            line(j + 1, begin)

        zz = z + (2 * lax.rem(q, 2) - 1) * j
        yy = y if Y == 1 else jnp.where(q < 2, y, 1 - y)
        slot = zz * Y + yy
        inside = jnp.logical_and(zz >= 0, zz < Z)
        inside = jnp.logical_and(inside, jnp.logical_or(j > 0, lax.rem(q, 2) == 1))

        @pl.when(inside)
        def _():
            if Y == 2:
                @pl.when(q >= 2)
                def _():
                    landed(k, slot)
                    cross(j, slot, lambda copy: copy.start())

            landed(sib, slot)
            process(slot)

        return c

    lax.fori_loop(0, Z * quarters, gather, 0)

    def share(buffer, count, ssem, rsem):
        def piece(slot):
            return buffer.at[slot] if count is None else buffer.at[slot, pl.ds(0, count)]

        def copy(p):
            peer = lax.rem(mine + p, nd)
            return remote(
                piece(mine), piece(mine), ssem.at[p], rsem.at[mine], peer // 2, lax.rem(peer, 2)
            )

        def start(p, c):
            copy(p).start()
            return c

        def wait_in(p, c):
            src = lax.rem(mine + p, nd)
            remote(
                piece(src), piece(src), ssem.at[p], rsem.at[src], me, sib
            ).wait_recv()
            return c

        def wait_out(p, c):
            copy(p).wait_send()
            return c

        return (
            lambda: lax.fori_loop(1, nd, start, 0),
            lambda: lax.fori_loop(1, nd, wait_in, 0),
            lambda: lax.fori_loop(1, nd, wait_out, 0),
        )

    start1, in1, out1 = share(stat1, None, ssend.at[0], srecv.at[0])
    start1()
    lax.fori_loop(1, n, meta_start, 0)
    lax.fori_loop(1, n, meta_wait, 0)
    counts = meta_all[:, 1, :]
    valid_total = jnp.sum(counts[:, 0:1], axis=0, keepdims=True)

    def combine(stat):
        peak = stat[0, 0]
        for d in range(1, nd):
            peak = jnp.maximum(peak, stat[d, 0])
        total = jnp.zeros_like(peak)
        for d in range(nd):
            total = total + stat[d, 1] * jnp.exp(stat[d, 0] - peak)
        b_scr[...] = jnp.exp(stat[mine, 0] - peak) / total
        return peak, total

    row_number = lax.broadcasted_iota(jnp.int32, (rows_n, 1), 0).astype(F32)

    def residuals(first):
        def go(i, acc):
            valid = (row_number < meta_all[i, 1:2, 0:1]).astype(F32) / valid_total
            target = column(meta_all[i, 0:1, :])
            probability = e_scr[rows(i), :] * column(b_scr[pl.ds(i, 1), :])
            is_label = (class_float == target).astype(F32)
            r_scr[rows(i), :] = (valid * (probability - is_label)).astype(BF16)
            if first:
                fw = (valid * probability * (1.0 - probability)).astype(BF16)
                fw_scr[rows(i), :] = fw
                row_sum = jnp.sum(fw.astype(F32), axis=1, keepdims=True)
                acc = acc + jnp.sum(row_sum * ssq[rows(i), 0:1], axis=0, keepdims=True)
            return acc

        return lax.fori_loop(0, n, go, jnp.zeros((1, 1), F32), unroll=4)

    in1()
    combine(stat1)
    fisher_part = residuals(True)
    damp_all[mine] = jnp.broadcast_to(fisher_part, damp_all.shape[1:])
    start_d, in_d, out_d = share(damp_all, None, dsend, drecv)
    start_d()

    step = min(512, half)
    per_half = half // step

    def chunk(i):
        return i // per_half, pl.ds(pl.multiple_of(lax.rem(i, per_half) * step, step), step)

    def gradient(i, c):
        h, part = chunk(i)
        g_scr[h, part, :] = jnp.dot(xt[h, part, :], r_scr[...], preferred_element_type=F32)
        return c

    lax.fori_loop(0, 2 * per_half, gradient, 0, unroll=2)

    in_d()
    fisher_sum = damp_all[0, 0:1, 0:1]
    for d in range(1, nd):
        fisher_sum = fisher_sum + damp_all[d, 0:1, 0:1]
    damping = DAMPING_SHARE * fisher_sum / scale + EPSILON
    e_scr[...] = jnp.zeros_like(e_scr)

    big = min(1024, half)
    parts = half // big

    def fisher_step(i, c):
        h = i // parts
        part = pl.ds(pl.multiple_of(lax.rem(i, parts) * big, big), big)
        block = xt[h, part, :]
        fisher = jnp.dot(block * block, fw_scr[...], preferred_element_type=F32)
        inverse = 1.0 / (fisher + damping)
        rec[h, part, :] = inverse
        change = g_scr[h, part, :] * inverse
        g_scr[h, part, :] = change
        low = (w[h, part, :] - LEARNING_RATE * change).astype(BF16)
        wlow[h, part, :] = low
        e_scr[...] += jnp.dot(x[h, :, part], low, preferred_element_type=F32)
        return c

    lax.fori_loop(0, 2 * parts, fisher_step, 0)

    def second(i, c):
        statistics(i, e_scr[rows(i), :], stat2, True)
        return c

    lax.fori_loop(0, n, second, 0, unroll=4)
    start2, in2, out2 = share(stat2, None, ssend.at[1], srecv.at[1])
    start2()
    in2()
    peak, total = combine(stat2)
    label = stat2[0, 2]
    for d in range(1, nd):
        label = label + stat2[d, 2]
    lane_row = lax.broadcasted_iota(jnp.int32, (n, rows_n), 1).astype(F32)
    loss_scr[...] = (lane_row < counts).astype(F32) * (peak + jnp.log(total) - label)
    losses[...] = loss_scr[pl.ds(me, 1), :]
    residuals(False)

    def place(i):
        h = jnp.where(i < per_half, sib, k)
        return h, pl.ds(pl.multiple_of(lax.rem(i, per_half) * step, step), step)

    def out_remote(i):
        h, part = place(i)
        return remote(
            w.at[h, part, :], moved.at[part, columns(k)], osend.at[i], orecv.at[i], me, sib
        )

    def out_local(i):
        h, part = place(i)
        return pltpu.make_async_copy(
            w.at[h, part, :], moved.at[part, columns(k)], out_sem.at[i - per_half]
        )

    def last(i, c):
        h, part = place(i)
        grad = jnp.dot(xt[h, part, :], r_scr[...], preferred_element_type=F32)
        w[h, part, :] = -g_scr[h, part, :] - grad * rec[h, part, :]

        @pl.when(i < per_half)
        def _():
            out_remote(i).start()

        @pl.when(i >= per_half)
        def _():
            out_local(i).start()

        return c

    w_send.wait_send()
    lax.fori_loop(0, 2 * per_half, last, 0)

    line(0, finish, own=True)

    def drain(j, c):
        line(j, finish)
        return c

    lax.fori_loop(1, Z, drain, 0)
    if Y == 2:
        def drain_side(zz, c):
            slot = zz * Y + (1 - y)
            cross(jnp.abs(zz - z), slot, lambda copy: copy.wait_send())
            return c

        lax.fori_loop(0, Z, drain_side, 0)

    def meta_done(p, c):
        meta_copy(p)[1].wait_send()
        return c

    lax.fori_loop(1, n, meta_done, 0)
    out1()
    out_d()
    out2()

    def out_done(i, c):
        out_remote(i).wait_send()
        _, part = place(i)
        remote(
            w.at[k, part, :], moved.at[part, columns(sib)], osend.at[i], orecv.at[i], me, sib
        ).wait_recv()
        out_local(i + per_half).wait()
        return c

    lax.fori_loop(0, per_half, out_done, 0)


def solution(mesh):
    n = mesh.shape["example"]
    Y = 2 if n == 8 else 1
    Z = n // Y
    nd = 2 * n

    def body(features, weights, labels, counts, active):
        rows_n, half = features.shape
        local = weights.shape[1]
        ck = local // 2
        all_rows = rows_n * n
        target = (labels % active[0]).astype(F32)
        meta = jnp.concatenate(
            [
                target[None, :],
                jnp.broadcast_to(counts.astype(F32)[:, None], (7, rows_n)),
            ],
            axis=0,
        )
        scale = float(half * 2 * local * n)
        per_half = half // min(512, half)
        dma = pltpu.SemaphoreType.DMA
        moved, losses = pl.pallas_call(
            functools.partial(kernel, Z, Y, scale),
            out_shape=(
                jax.ShapeDtypeStruct(weights.shape, F32),
                jax.ShapeDtypeStruct((1, rows_n), F32),
            ),
            in_specs=[
                pl.BlockSpec(memory_space=pl.ANY),
                pl.BlockSpec(memory_space=pl.ANY),
                pl.BlockSpec(memory_space=pltpu.VMEM),
                pl.BlockSpec(memory_space=pltpu.SMEM),
            ],
            out_specs=(
                pl.BlockSpec(memory_space=pl.ANY),
                pl.BlockSpec(memory_space=pltpu.VMEM),
            ),
            scratch_shapes=[
                pltpu.VMEM((2, all_rows, half), BF16),
                pltpu.VMEM((2, half, all_rows), BF16),
                pltpu.VMEM((2, half, ck), F32),
                pltpu.VMEM((2, half, ck), BF16),
                pltpu.VMEM((all_rows, ck), F32),
                pltpu.VMEM((all_rows, ck), BF16),
                pltpu.VMEM((all_rows, ck), BF16),
                pltpu.VMEM((2, half, ck), F32),
                pltpu.VMEM((2, half, ck), F32),
                pltpu.VMEM((n, 8, rows_n), F32),
                pltpu.VMEM((nd, 2, n, rows_n), F32),
                pltpu.VMEM((nd, 3, n, rows_n), F32),
                pltpu.VMEM((nd, 8, 128), F32),
                pltpu.VMEM((n, rows_n), F32),
                pltpu.VMEM((all_rows, 128), F32),
                pltpu.VMEM((n, rows_n), F32),
                dma, dma,
                dma((4, n)), dma((2, n)),
                dma, dma,
                dma((n,)), dma((n,)),
                dma((2, nd)), dma((2, nd)),
                dma((nd,)), dma((nd,)),
                dma((per_half,)), dma((per_half,)), dma((per_half,)),
            ],
            compiler_params=pltpu.CompilerParams(
                collective_id=0, has_side_effects=True, vmem_limit_bytes=67043328
            ),
        )(features, weights, meta, active)
        return moved, losses.reshape(rows_n)

    return jax.shard_map(
        body,
        mesh=mesh,
        in_specs=(
            P(("groups", "example"), "cls"),
            P(("groups", "cls"), "example"),
            P(("groups", "example")),
            P(("groups", "example")),
            P("groups"),
        ),
        out_specs=(P(("groups", "cls"), "example"), P(("groups", "example"))),
        check_vma=False,
    )
```
